512 devices in a mesh: seq: 64 (over y, z), tensor: 8 (over x, core).
Axes of the slice: x: 4, y: 8, z: 8, core: 2. Of those that a mesh axis runs over, the one named last changes fastest.
Arguments:
- query_rows: bfloat16 [8192, 4096], P('seq', 'tensor'), may hold values from -6 to 6
- key_rows: bfloat16 [8192, 4096], P('seq', 'tensor'), may hold values from -6 to 6
- value_rows: bfloat16 [8192, 4096], P('seq', 'tensor'), may hold values from -6 to 6
- block_mask: int32 [64, 1], P('seq'), may hold values 0 or 1
- norm_gain: float32 [4096], P('tensor'), may hold values from 0.1 to 1.9
- out_weight: bfloat16 [4096, 4096], P('tensor'), may hold values from -0.125 to 0.125
Outputs:
- mixed: bfloat16 [8192, 4096], P('seq', 'tensor')
The draws below stay inside these ranges and needn't reach their ends.
All inputs are finite; a program needn't handle non-finite values. No bound on the sum of `block_mask` on one device may be relied on, other than what follows from the above.
Results may differ from the reference program's by a relative error of at most 0.014.
Values may be sent and summed in bfloat16 or wider, within the bound.
A program may use at most 64 MiB of HBM per device.

```python
import jax
import jax.numpy as jnp
from jax import lax

D = 4096
H = 32
DH = 128
HD = 4096
TOK_DEV = 128
BLK = 128
TOKENS = 8192
N_SEQ = 64
N_TENSOR = 8


def with_ends(result, key, least, high):
    place = [jax.random.randint(jax.random.fold_in(key, axis), (), 0, length) for axis, length in enumerate(result.shape)]
    widest = result.shape.index(max(result.shape))
    next_to = place[:widest] + [(place[widest] + 1) % result.shape[widest]] + place[widest + 1:]
    return result.at[tuple(place)].set(least).at[tuple(next_to)].set(high)


def with_spikes(result, own_key, source, target, blocks, factor):
    def block_of(dim):
        return (jnp.arange(result.shape[dim]) // (result.shape[dim] // blocks)).reshape((-1,) + (1,) * (result.ndim - 1 - dim))

    near = jax.random.permutation(own_key, blocks)[block_of(target)]
    other_side = (block_of(target) + blocks // 2) % blocks
    return jnp.where((block_of(source) == near) | (block_of(source) == other_side), factor * result, result)


def shard_levels(own_key, extent, shards, smallest, largest):
    gain, own = 1.0, jax.random.fold_in(own_key, 6)
    for position, shards_of in shards:
        draws = jnp.exp(jax.random.uniform(jax.random.fold_in(own, position), (shards_of,), jnp.float32, smallest / len(shards), largest / len(shards)))
        gain = gain * jnp.repeat(draws, extent[position] // shards_of).reshape([-1 if axis == position else 1 for axis in range(len(extent))])
    return gain


def bell_draw(stream_key, shape, deviation, most, shards=(), kind=jnp.bfloat16):
    array = deviation * jax.random.normal(stream_key, shape, jnp.float32)
    if shards:
        array = array * shard_levels(stream_key, shape, shards, -0.22, 0.18)
    return jnp.clip(array, -most, most).astype(kind)


def noise_with(own_key, extent, scale, most, split, heavy, dtype=jnp.bfloat16):
    entries = scale * jax.random.normal(own_key, extent, jnp.float32)
    if split:
        entries = entries * shard_levels(own_key, extent, split, -0.22, 0.18)
    return jnp.clip(with_spikes(entries, jax.random.fold_in(own_key, 3), *heavy), -most, most).astype(dtype)


def setup_inputs(seed: int = 0) -> dict:
    streams_of = jax.random.split(jax.random.key(seed), 7)
    query_rows = bell_draw(streams_of[0], (TOKENS, HD), 1.0, 6.0, ((0, 64), (1, 8)))
    key_rows = bell_draw(streams_of[1], (TOKENS, HD), 1.0, 6.0, ((0, 64), (1, 8)))
    value_rows = bell_draw(streams_of[2], (TOKENS, HD), 1.0, 6.0, ((0, 64), (1, 8)))
    block_mask = with_ends((jax.random.randint(streams_of[3], (TOKENS // BLK, TOK_DEV // BLK), 0, 4) < 3).astype(jnp.int32), jax.random.fold_in(streams_of[3], 1), 0, 1)
    norm_gain = jnp.clip(1.0 + 0.18 * jax.random.normal(streams_of[4], (HD,), jnp.float32), 0.1, 1.9)
    out_weight = noise_with(streams_of[5], (HD, D), HD ** -0.5, 0.125, ((0, 8),), (0, 1, 8, 2.0))
    return dict(query_rows=query_rows, key_rows=key_rows, value_rows=value_rows, block_mask=block_mask, norm_gain=norm_gain, out_weight=out_weight)


def reference(query_rows, key_rows, value_rows, block_mask, norm_gain, out_weight):
    blocks = TOK_DEV // BLK
    queries = query_rows.reshape(N_SEQ, TOK_DEV, H, DH)
    keyset = key_rows.reshape(N_SEQ, TOK_DEV, H, DH)
    valueset = value_rows.reshape(N_SEQ, TOK_DEV, H, DH)
    masks = block_mask.reshape(N_SEQ, blocks, blocks)

    def group_state(pair):
        return jnp.einsum('thd,the->hde', pair[0].astype(jnp.float32), pair[1].astype(jnp.float32))
    states = lax.map(group_state, (keyset, valueset))
    running = jnp.cumsum(states, axis=0)
    prefix = jnp.concatenate([jnp.zeros((1, H, DH, DH), jnp.float32), running[:-1]], axis=0)
    row_pos = lax.broadcasted_iota(jnp.int32, (TOK_DEV, TOK_DEV), 0)
    col_pos = lax.broadcasted_iota(jnp.int32, (TOK_DEV, TOK_DEV), 1)

    def group_out(items):
        query_blk, key_blk, value_blk, mask_blk, prefix_blk = items
        scores = jnp.einsum('thd,shd->hts', query_blk.astype(jnp.float32), key_blk.astype(jnp.float32))
        expanded = jnp.repeat(jnp.repeat(mask_blk, BLK, axis=0), BLK, axis=1)
        allowed = (expanded > 0) & (col_pos <= row_pos)
        weights = jnp.where(allowed[None], scores, 0.0).astype(jnp.bfloat16)
        intra = jnp.einsum('hts,she->the', weights.astype(jnp.float32), value_blk.astype(jnp.float32))
        inter = jnp.einsum('thd,hde->the', query_blk.astype(jnp.float32), prefix_blk, precision=lax.Precision.HIGHEST)
        return intra + inter
    attn = lax.map(group_out, (queries, keyset, valueset, masks, prefix)).reshape(TOKENS, H, DH)
    meansq = lax.optimization_barrier(jnp.mean(attn * attn, axis=-1, keepdims=True))
    normed = attn * lax.rsqrt(meansq + 1e-05) * norm_gain.reshape(H, DH)
    gated = normed.reshape(TOKENS, HD).astype(jnp.bfloat16)
    width = HD // N_TENSOR
    total = jnp.zeros((TOKENS, D), jnp.float32)
    for group in range(N_TENSOR):
        part = jnp.dot(gated[:, group * width:(group + 1) * width], out_weight[group * width:(group + 1) * width], preferred_element_type=jnp.float32).astype(jnp.bfloat16)
        part = lax.optimization_barrier(part)
        total = total + part.astype(jnp.float32)
    return total.astype(jnp.bfloat16)
```

```python
import functools
import math

import jax
import jax.numpy as jnp
from jax import lax
from jax.experimental import pallas as pl
from jax.experimental.pallas import tpu as pltpu
from jax.sharding import PartitionSpec as P

DH = 128
F32, BF16 = jnp.float32, jnp.bfloat16
MESH = pl.DeviceIdType.MESH
PARTS = 2


def far_first(n):
    return sorted(range(1, n), key=lambda k: -min(k, n - k))


def kernel(ny, nz, nx, q_hbm, k_hbm, v_hbm, m_hbm, g_hbm, w_hbm, out_ref, q, k, v, m, g, w, state, rows, before, total,
           cols, ready, prefix, intra, gated, mine, pair_out, pair_in, chip_out, chip_in, load_sem, wload_sem, sa, ra, sb, rb,
           sc, rc, sp, rp, sx, rx):
    tok, feat = q.shape
    heads = feat // DH
    sl = DH // nz
    lw = feat // PARTS
    width = w.shape[2]
    seq, ten = lax.axis_index("seq"), lax.axis_index("tensor")
    y, z = seq // nz, lax.rem(seq, nz)
    x, c = ten // 2, lax.rem(ten, 2)

    def row_peer(j):
        pz = lax.rem(z + j, nz)
        return pz, (y * nz + pz, ten)

    def col_peer(j):
        py = lax.rem(y + j, ny)
        return py, (py * nz + z, ten)

    def chip_peer(j):
        px = lax.rem(x + j, nx)
        return px, (seq, px * 2 + c)

    partner = (seq, x * 2 + (1 - c))

    loads = [pltpu.make_async_copy(a, b, load_sem.at[i]) for i, (a, b) in enumerate(
        ((k_hbm, k), (v_hbm, v), (q_hbm, q), (m_hbm, m), (g_hbm, g)))]
    for copy in loads:
        copy.start()
    hops = far_first(nx) + [0]
    wloads = []
    for i, j in enumerate(hops):
        px, _ = chip_peer(j)
        for half, core in ((0, 1 - c), (1, c)):
            columns = pl.ds(pl.multiple_of((px * 2 + core) * width, width), width)
            copy = pltpu.make_async_copy(w_hbm.at[:, columns], w.at[2 * i + half], wload_sem.at[2 * i + half])
            copy.start()
            wloads.append(copy)

    cols[...] = jnp.zeros_like(cols)
    barrier = pltpu.get_barrier_semaphore()
    peers = [row_peer(j)[1] for j in far_first(nz)] + [col_peer(j)[1] for j in far_first(ny)]
    peers += [chip_peer(j)[1] for j in far_first(nx)] + [partner]
    for peer in peers:
        pl.semaphore_signal(barrier, inc=1, device_id=peer, device_id_type=MESH)

    loads[0].wait()
    loads[1].wait()
    for h in range(heads):
        one = lax.dot_general(k[:, h * DH:(h + 1) * DH], v[:, h * DH:(h + 1) * DH], (((0,), (0,)), ((), ())),
                              preferred_element_type=F32)
        part, at = divmod(h * DH, lw)
        state[part, :, :, at:at + DH] = one.astype(BF16).reshape(nz, sl, DH)
    pl.semaphore_wait(barrier, len(peers))

    sends = []

    def send(src, dst, send_sem, recv_sem, device):
        copy = pltpu.make_async_remote_copy(src_ref=src, dst_ref=dst, send_sem=send_sem, recv_sem=recv_sem, device_id=device,
                                            device_id_type=MESH)
        copy.start()
        return copy

    def arrived(dst, recv_sem, send_sem, device):
        pltpu.make_async_remote_copy(src_ref=dst, dst_ref=dst, send_sem=send_sem, recv_sem=recv_sem, device_id=device,
                                     device_id_type=MESH).wait_recv()

    for p in range(PARTS):
        for j in far_first(nz):
            pz, device = row_peer(j)
            sends.append(send(state.at[p, pz], rows.at[p, z], sa.at[p, j], ra.at[p, z], device))
    for p in range(PARTS):
        rows[p, z] = state[p, z]

    for copy in loads[2:]:
        copy.wait()
    row_pos = lax.broadcasted_iota(jnp.int32, (tok, tok), 0)
    col_pos = lax.broadcasted_iota(jnp.int32, (tok, tok), 1)
    allowed = (jnp.full((tok, tok), m[0, 0], jnp.int32) > 0) & (col_pos <= row_pos)
    for h in range(heads):
        at = slice(h * DH, (h + 1) * DH)
        scores = lax.dot_general(q[:, at], k[:, at], (((1,), (1,)), ((), ())), preferred_element_type=F32)
        weights = jnp.where(allowed, scores, 0.0).astype(BF16)
        intra[:, at] = jnp.dot(weights, v[:, at], preferred_element_type=F32)

    for p in range(PARTS):
        for j in far_first(nz)[::-1]:
            pz, device = row_peer(j)
            arrived(rows.at[p, pz], ra.at[p, pz], sa.at[p, j], device)
        run = jnp.zeros((sl, lw), F32)
        for i in range(nz):
            before[p, i] = run
            run = run + rows[p, i].astype(F32)
        total[p] = run.astype(BF16)
        for j in range(ny - 1, 0, -1):
            @pl.when(y + j < ny)
            def _():
                send(total.at[p], cols.at[p, y], sb.at[p, j], rb.at[p, y], ((y + j) * nz + z, ten))

    for p in range(PARTS):
        for j in range(1, ny):
            @pl.when(y - j >= 0)
            def _():
                arrived(cols.at[p, y - j], rb.at[p, y - j], sb.at[p, j], ((y - j) * nz + z, ten))
        base = jnp.zeros((sl, lw), F32)
        for i in range(ny):
            base = base + cols[p, i].astype(F32)
        for i in range(nz):
            ready[p, i] = (base + before[p, i]).astype(BF16)
        for j in far_first(nz):
            pz, device = row_peer(j)
            sends.append(send(ready.at[p, pz], prefix.at[p, z], sc.at[p, j], rc.at[p, z], device))
        prefix[p, z] = ready[p, z]

    for p in range(PARTS):
        for j in far_first(nz)[::-1]:
            pz, device = row_peer(j)
            arrived(prefix.at[p, pz], rc.at[p, pz], sc.at[p, j], device)
        for h in range(heads // PARTS):
            at = slice(p * lw + h * DH, p * lw + (h + 1) * DH)
            one = prefix[p, :, :, h * DH:(h + 1) * DH].reshape(DH, DH)
            attn = intra[:, at] + jnp.dot(q[:, at], one, preferred_element_type=F32)
            meansq = jnp.mean(attn * attn, axis=-1, keepdims=True)
            gated[:, at] = (attn * lax.rsqrt(meansq + 1e-05) * g[:, at]).astype(BF16)

    for i, j in enumerate(hops):
        wloads[2 * i].wait()
        pair_out[i] = jnp.dot(gated[...], w[2 * i], preferred_element_type=F32).astype(BF16)
        sends.append(send(pair_out.at[i], pair_in.at[i], sp.at[i], rp.at[i], partner))
        wloads[2 * i + 1].wait()
        mine[i] = jnp.dot(gated[...], w[2 * i + 1], preferred_element_type=F32)
    for i, j in enumerate(hops):
        arrived(pair_in.at[i], rp.at[i], sp.at[i], partner)
        if j:
            chip_out[i] = (mine[i] + pair_in[i].astype(F32)).astype(BF16)
            sends.append(send(chip_out.at[i], chip_in.at[i], sx.at[i], rx.at[i], chip_peer(j)[1]))
    result = mine[len(hops) - 1] + pair_in[len(hops) - 1].astype(F32)
    for i, j in enumerate(hops[:-1]):
        arrived(chip_in.at[i], rx.at[i], sx.at[i], chip_peer(j)[1])
        result = result + chip_in[i].astype(F32)
    out_ref[...] = result.astype(BF16)

    for copy in sends:
        copy.wait_send()
    for p in range(PARTS):
        for j in range(1, ny):
            @pl.when(y + j < ny)
            def _():
                pltpu.make_async_remote_copy(src_ref=total.at[p], dst_ref=cols.at[p, y], send_sem=sb.at[p, j],
                                             recv_sem=rb.at[p, y], device_id=((y + j) * nz + z, ten),
                                             device_id_type=MESH).wait_send()


def solution(mesh):
    n_seq, n_ten = mesh.shape["seq"], mesh.shape["tensor"]
    nz = math.isqrt(n_seq)
    ny, nx = n_seq // nz, n_ten // 2

    def local(query_rows, key_rows, value_rows, block_mask, norm_gain, out_weight):
        tok, feat = query_rows.shape
        width = out_weight.shape[1] // n_ten
        sl, lw = DH // nz, feat // PARTS
        dma = pltpu.SemaphoreType.DMA
        slices = pltpu.VMEM((PARTS, nz, sl, lw), BF16)
        return pl.pallas_call(
            functools.partial(kernel, ny, nz, nx),
            out_shape=jax.ShapeDtypeStruct((tok, width), BF16),
            in_specs=[pl.BlockSpec(memory_space=pl.ANY)] * 6,
            out_specs=pl.BlockSpec(memory_space=pltpu.VMEM),
            scratch_shapes=[
                pltpu.VMEM((tok, feat), BF16), pltpu.VMEM((tok, feat), BF16), pltpu.VMEM((tok, feat), BF16),
                pltpu.SMEM((1, 1), jnp.int32), pltpu.VMEM((1, feat), F32),
                pltpu.VMEM((2 * nx, feat, width), BF16),
                slices, slices, pltpu.VMEM((PARTS, nz, sl, lw), F32), pltpu.VMEM((PARTS, sl, lw), BF16),
                pltpu.VMEM((PARTS, ny, sl, lw), BF16), slices, slices,
                pltpu.VMEM((tok, feat), F32), pltpu.VMEM((tok, feat), BF16),
                pltpu.VMEM((nx, tok, width), F32), pltpu.VMEM((nx, tok, width), BF16), pltpu.VMEM((nx, tok, width), BF16),
                pltpu.VMEM((nx, tok, width), BF16), pltpu.VMEM((nx, tok, width), BF16),
                dma((5,)), dma((2 * nx,)), dma((PARTS, nz)), dma((PARTS, nz)), dma((PARTS, ny)), dma((PARTS, ny)),
                dma((PARTS, nz)), dma((PARTS, nz)), dma((nx,)), dma((nx,)), dma((nx,)), dma((nx,)),
            ],
            compiler_params=pltpu.CompilerParams(collective_id=0, has_side_effects=True),
        )(query_rows, key_rows, value_rows, block_mask, norm_gain.reshape(1, feat), out_weight)

    placed = (P("seq", "tensor"), P("seq", "tensor"), P("seq", "tensor"), P("seq", None), P("tensor"), P("tensor", None))
    return jax.shard_map(local, mesh=mesh, in_specs=placed, out_specs=P("seq", "tensor"), check_vma=False)
```

```python
import functools
import math

import jax
import jax.numpy as jnp
from jax import lax
from jax.experimental import pallas as pl
from jax.experimental.pallas import tpu as pltpu
from jax.sharding import PartitionSpec as P

DH = 128
F32, BF16 = jnp.float32, jnp.bfloat16
MESH = pl.DeviceIdType.MESH
PARTS = 2


def far_first(n):
    return sorted(range(1, n), key=lambda k: -min(k, n - k))


def kernel(ny, nz, nx, q_hbm, k_hbm, v_hbm, m_hbm, g_hbm, w_hbm, out_ref, q, k, v, m, g, w, w_in, state, rows, before, total,
           cols, ready, prefix, intra, gated, gated_in, relay_out, relay_in, chip_out, chip_in, load_sem, wload_sem, sa, ra, sb,
           rb, sc, rc, sw, rw, sg, rg, sr, rr, sx, rx):
    tok, feat = q.shape
    heads = feat // DH
    sl = DH // nz
    lw = feat // PARTS
    width = w.shape[2]
    half = width // 2
    seq, ten = lax.axis_index("seq"), lax.axis_index("tensor")
    y, z = seq // nz, lax.rem(seq, nz)
    x, c = ten // 2, lax.rem(ten, 2)

    def row_peer(j):
        pz = lax.rem(z + j, nz)
        return pz, (y * nz + pz, ten)

    def col_peer(j):
        py = lax.rem(y + j, ny)
        return py, (py * nz + z, ten)

    def chip_peer(j):
        px = lax.rem(x + j, nx)
        return px, (seq, px * 2 + c)

    partner = (seq, x * 2 + (1 - c))

    loads = [pltpu.make_async_copy(a, b, load_sem.at[i]) for i, (a, b) in enumerate(
        ((k_hbm, k), (v_hbm, v), (q_hbm, q), (m_hbm, m), (g_hbm, g)))]
    for copy in loads:
        copy.start()
    hops = (2, 1, nx - 1, 0)

    def block(i, core):
        px, _ = chip_peer(hops[i])
        return w_hbm.at[:, pl.ds(pl.multiple_of((px * 2 + core) * width, width), width)]

    wloads = [pltpu.make_async_copy(block(i, c), w.at[i], wload_sem.at[i]) for i in range(nx)]
    for copy in wloads:
        copy.start()

    cols[...] = jnp.zeros_like(cols)
    barrier = pltpu.get_barrier_semaphore()
    peers = [row_peer(j)[1] for j in far_first(nz)] + [col_peer(j)[1] for j in far_first(ny)]
    ahead, behind = chip_peer(1)[1], chip_peer(nx - 1)[1]
    peers += [ahead, behind, partner]
    for peer in peers:
        pl.semaphore_signal(barrier, inc=1, device_id=peer, device_id_type=MESH)

    loads[0].wait()
    loads[1].wait()
    for h in range(heads):
        one = lax.dot_general(k[:, h * DH:(h + 1) * DH], v[:, h * DH:(h + 1) * DH], (((0,), (0,)), ((), ())),
                              preferred_element_type=F32)
        part, at = divmod(h * DH, lw)
        state[part, :, :, at:at + DH] = one.astype(BF16).reshape(nz, sl, DH)
    pl.semaphore_wait(barrier, len(peers))

    sends = []

    def send(src, dst, send_sem, recv_sem, device):
        copy = pltpu.make_async_remote_copy(src_ref=src, dst_ref=dst, send_sem=send_sem, recv_sem=recv_sem, device_id=device,
                                            device_id_type=MESH)
        copy.start()
        return copy

    def arrived(dst, recv_sem, send_sem, device):
        pltpu.make_async_remote_copy(src_ref=dst, dst_ref=dst, send_sem=send_sem, recv_sem=recv_sem, device_id=device,
                                     device_id_type=MESH).wait_recv()

    for p in range(PARTS):
        for j in far_first(nz):
            pz, device = row_peer(j)
            sends.append(send(state.at[p, pz], rows.at[p, z], sa.at[p, j], ra.at[p, z], device))
    for i in range(nx):
        sends.append(send(block(i, 1 - c), w_in.at[i], sw.at[i], rw.at[i], partner))
    for p in range(PARTS):
        rows[p, z] = state[p, z]

    for copy in loads[2:]:
        copy.wait()
    row_pos = lax.broadcasted_iota(jnp.int32, (tok, tok), 0)
    col_pos = lax.broadcasted_iota(jnp.int32, (tok, tok), 1)
    allowed = (jnp.full((tok, tok), m[0, 0], jnp.int32) > 0) & (col_pos <= row_pos)
    for h in range(heads):
        at = slice(h * DH, (h + 1) * DH)
        scores = lax.dot_general(q[:, at], k[:, at], (((1,), (1,)), ((), ())), preferred_element_type=F32)
        weights = jnp.where(allowed, scores, 0.0).astype(BF16)
        intra[:, at] = jnp.dot(weights, v[:, at], preferred_element_type=F32)

    for p in range(PARTS):
        for j in far_first(nz)[::-1]:
            pz, device = row_peer(j)
            arrived(rows.at[p, pz], ra.at[p, pz], sa.at[p, j], device)
        run = jnp.zeros((sl, lw), F32)
        for i in range(nz):
            before[p, i] = run
            run = run + rows[p, i].astype(F32)
        total[p] = run.astype(BF16)
        for j in range(ny - 1, 0, -1):
            @pl.when(y + j < ny)
            def _():
                send(total.at[p], cols.at[p, y], sb.at[p, j], rb.at[p, y], ((y + j) * nz + z, ten))

    for p in range(PARTS):
        for j in range(1, ny):
            @pl.when(y - j >= 0)
            def _():
                arrived(cols.at[p, y - j], rb.at[p, y - j], sb.at[p, j], ((y - j) * nz + z, ten))
        base = jnp.zeros((sl, lw), F32)
        for i in range(ny):
            base = base + cols[p, i].astype(F32)
        for i in range(nz):
            ready[p, i] = (base + before[p, i]).astype(BF16)
        for j in far_first(nz):
            pz, device = row_peer(j)
            sends.append(send(ready.at[p, pz], prefix.at[p, z], sc.at[p, j], rc.at[p, z], device))
        prefix[p, z] = ready[p, z]

    for p in range(PARTS):
        for j in far_first(nz)[::-1]:
            pz, device = row_peer(j)
            arrived(prefix.at[p, pz], rc.at[p, pz], sc.at[p, j], device)
        for h in range(heads // PARTS):
            at = slice(p * lw + h * DH, p * lw + (h + 1) * DH)
            one = prefix[p, :, :, h * DH:(h + 1) * DH].reshape(DH, DH)
            attn = intra[:, at] + jnp.dot(q[:, at], one, preferred_element_type=F32)
            meansq = jnp.mean(attn * attn, axis=-1, keepdims=True)
            gated[:, at] = (attn * lax.rsqrt(meansq + 1e-05) * g[:, at]).astype(BF16)
        at = pl.ds(p * lw, lw)
        sends.append(send(gated.at[:, at], gated_in.at[:, at], sg.at[p], rg.at[p], partner))

    def partial(i, part):
        at = slice(part * half, (part + 1) * half)
        return (jnp.dot(gated[...], w[i, :, at], preferred_element_type=F32) +
                jnp.dot(gated_in[...], w_in[i, :, at], preferred_element_type=F32))

    def there(i):
        wloads[i].wait()
        arrived(w_in.at[i], rw.at[i], sw.at[i], partner)

    there(0)
    for p in range(PARTS):
        at = pl.ds(p * lw, lw)
        arrived(gated_in.at[:, at], rg.at[p], sg.at[p], partner)
    both = (ahead, behind)
    for d in range(2):
        relay_out[d] = partial(0, d).astype(BF16)
        sends.append(send(relay_out.at[d], relay_in.at[d], sr.at[d], rr.at[d], both[d]))
    for d in range(2):
        there(1 + d)
        chip_out[d, 1 - d] = partial(1 + d, 1 - d).astype(BF16)
        sends.append(send(chip_out.at[d, 1 - d], chip_in.at[d, 1 - d], sx.at[d, 1 - d], rx.at[d, 1 - d], both[d]))
    for d in range(2):
        term = partial(1 + d, d)
        arrived(relay_in.at[d], rr.at[d], sr.at[d], both[1 - d])
        chip_out[d, d] = (term + relay_in[d].astype(F32)).astype(BF16)
        sends.append(send(chip_out.at[d, d], chip_in.at[d, d], sx.at[d, d], rx.at[d, d], both[d]))
    there(3)
    own = [partial(3, part) for part in range(2)]
    for d in range(2):
        arrived(chip_in.at[d, 1 - d], rx.at[d, 1 - d], sx.at[d, 1 - d], both[1 - d])
        own[1 - d] = own[1 - d] + chip_in[d, 1 - d].astype(F32)
    for d in range(2):
        arrived(chip_in.at[d, d], rx.at[d, d], sx.at[d, d], both[1 - d])
        out_ref[:, d * half:(d + 1) * half] = (own[d] + chip_in[d, d].astype(F32)).astype(BF16)

    for copy in sends:
        copy.wait_send()
    for p in range(PARTS):
        for j in range(1, ny):
            @pl.when(y + j < ny)
            def _():
                pltpu.make_async_remote_copy(src_ref=total.at[p], dst_ref=cols.at[p, y], send_sem=sb.at[p, j],
                                             recv_sem=rb.at[p, y], device_id=((y + j) * nz + z, ten),
                                             device_id_type=MESH).wait_send()


def solution(mesh):
    n_seq, n_ten = mesh.shape["seq"], mesh.shape["tensor"]
    nz = math.isqrt(n_seq)
    ny, nx = n_seq // nz, n_ten // 2

    def local(query_rows, key_rows, value_rows, block_mask, norm_gain, out_weight):
        tok, feat = query_rows.shape
        width = out_weight.shape[1] // n_ten
        sl, lw = DH // nz, feat // PARTS
        dma = pltpu.SemaphoreType.DMA
        slices = pltpu.VMEM((PARTS, nz, sl, lw), BF16)
        return pl.pallas_call(
            functools.partial(kernel, ny, nz, nx),
            out_shape=jax.ShapeDtypeStruct((tok, width), BF16),
            in_specs=[pl.BlockSpec(memory_space=pl.ANY)] * 6,
            out_specs=pl.BlockSpec(memory_space=pltpu.VMEM),
            scratch_shapes=[
                pltpu.VMEM((tok, feat), BF16), pltpu.VMEM((tok, feat), BF16), pltpu.VMEM((tok, feat), BF16),
                pltpu.SMEM((1, 1), jnp.int32), pltpu.VMEM((1, feat), F32),
                pltpu.VMEM((nx, feat, width), BF16), pltpu.VMEM((nx, feat, width), BF16),
                slices, slices, pltpu.VMEM((PARTS, nz, sl, lw), F32), pltpu.VMEM((PARTS, sl, lw), BF16),
                pltpu.VMEM((PARTS, ny, sl, lw), BF16), slices, slices,
                pltpu.VMEM((tok, feat), F32), pltpu.VMEM((tok, feat), BF16), pltpu.VMEM((tok, feat), BF16),
                pltpu.VMEM((2, tok, width // 2), BF16), pltpu.VMEM((2, tok, width // 2), BF16),
                pltpu.VMEM((2, 2, tok, width // 2), BF16), pltpu.VMEM((2, 2, tok, width // 2), BF16),
                dma((5,)), dma((nx,)), dma((PARTS, nz)), dma((PARTS, nz)), dma((PARTS, ny)), dma((PARTS, ny)),
                dma((PARTS, nz)), dma((PARTS, nz)), dma((nx,)), dma((nx,)), dma((PARTS,)), dma((PARTS,)),
                dma((2,)), dma((2,)), dma((2, 2)), dma((2, 2)),
            ],
            compiler_params=pltpu.CompilerParams(collective_id=0, has_side_effects=True),
        )(query_rows, key_rows, value_rows, block_mask, norm_gain.reshape(1, feat), out_weight)

    placed = (P("seq", "tensor"), P("seq", "tensor"), P("seq", "tensor"), P("seq", None), P("tensor"), P("tensor", None))
    return jax.shard_map(local, mesh=mesh, in_specs=placed, out_specs=P("seq", "tensor"), check_vma=False)
```

```python
import functools
import math

import jax
import jax.numpy as jnp
from jax import lax
from jax.experimental import pallas as pl
from jax.experimental.pallas import tpu as pltpu
from jax.sharding import PartitionSpec as P

DH = 128
F32, BF16 = jnp.float32, jnp.bfloat16
MESH = pl.DeviceIdType.MESH
PARTS = 2
CHUNKS = 2


def far_first(n):
    return sorted(range(1, n), key=lambda k: -min(k, n - k))


def kernel(ny, nz, nx, q_hbm, k_hbm, v_hbm, m_hbm, g_hbm, w_hbm, out_ref, q, k, v, m, g, w, w_in, state, rows, before, total,
           cols, ready, prefix, intra, gated, gated_in, relay_out, relay_in, direct_out, direct_in, chip_out, chip_in,
           load_sem, wload_sem, sa, ra, sb, rb, sc, rc, sw, rw, sg, rg, sr, rr, sd, rd, sx, rx):
    tok, feat = q.shape
    heads = feat // DH
    sl = DH // nz
    lw = feat // PARTS
    width = w.shape[2]
    half = width // 2
    seq, ten = lax.axis_index("seq"), lax.axis_index("tensor")
    y, z = seq // nz, lax.rem(seq, nz)
    x, c = ten // 2, lax.rem(ten, 2)

    def row_peer(j):
        pz = lax.rem(z + j, nz)
        return pz, (y * nz + pz, ten)

    def col_peer(j):
        py = lax.rem(y + j, ny)
        return py, (py * nz + z, ten)

    def chip_peer(j):
        px = lax.rem(x + j, nx)
        return px, (seq, px * 2 + c)

    partner = (seq, x * 2 + (1 - c))

    cols[...] = jnp.zeros_like(cols)
    barrier = pltpu.get_barrier_semaphore()
    peers = [row_peer(j)[1] for j in far_first(nz)] + [col_peer(j)[1] for j in far_first(ny)]
    ahead, behind = chip_peer(1)[1], chip_peer(nx - 1)[1]
    peers += [ahead, behind, partner]
    for peer in peers:
        pl.semaphore_signal(barrier, inc=1, device_id=peer, device_id_type=MESH)

    loads = [pltpu.make_async_copy(a, b, load_sem.at[i]) for i, (a, b) in enumerate(
        ((k_hbm, k), (v_hbm, v), (q_hbm, q), (m_hbm, m), (g_hbm, g)))]
    for copy in loads:
        copy.start()
    hops = (2, 1, nx - 1, 0)

    def block(i, core):
        px, _ = chip_peer(hops[i])
        return w_hbm.at[:, pl.ds(pl.multiple_of((px * 2 + core) * width, width), width)]

    wloads = [pltpu.make_async_copy(block(i, c), w.at[i], wload_sem.at[i]) for i in range(nx)]
    for copy in wloads:
        copy.start()

    loads[0].wait()
    loads[1].wait()
    for h in range(heads):
        one = lax.dot_general(k[:, h * DH:(h + 1) * DH], v[:, h * DH:(h + 1) * DH], (((0,), (0,)), ((), ())),
                              preferred_element_type=F32)
        part, at = divmod(h * DH, lw)
        state[part, :, :, at:at + DH] = one.astype(BF16).reshape(nz, sl, DH)
    pl.semaphore_wait(barrier, len(peers))

    sends = []

    def send(src, dst, send_sem, recv_sem, device):
        copy = pltpu.make_async_remote_copy(src_ref=src, dst_ref=dst, send_sem=send_sem, recv_sem=recv_sem, device_id=device,
                                            device_id_type=MESH)
        copy.start()
        return copy

    def arrived(dst, recv_sem, send_sem, device):
        pltpu.make_async_remote_copy(src_ref=dst, dst_ref=dst, send_sem=send_sem, recv_sem=recv_sem, device_id=device,
                                     device_id_type=MESH).wait_recv()

    for p in range(PARTS):
        for j in far_first(nz):
            pz, device = row_peer(j)
            sends.append(send(state.at[p, pz], rows.at[p, z], sa.at[p, j], ra.at[p, z], device))
    for i in range(nx):
        sends.append(send(block(i, 1 - c), w_in.at[i], sw.at[i], rw.at[i], partner))
    for p in range(PARTS):
        rows[p, z] = state[p, z]

    for copy in loads[2:]:
        copy.wait()
    row_pos = lax.broadcasted_iota(jnp.int32, (tok, tok), 0)
    col_pos = lax.broadcasted_iota(jnp.int32, (tok, tok), 1)
    allowed = (jnp.full((tok, tok), m[0, 0], jnp.int32) > 0) & (col_pos <= row_pos)
    for h in range(heads):
        at = slice(h * DH, (h + 1) * DH)
        scores = lax.dot_general(q[:, at], k[:, at], (((1,), (1,)), ((), ())), preferred_element_type=F32)
        weights = jnp.where(allowed, scores, 0.0).astype(BF16)
        intra[:, at] = jnp.dot(weights, v[:, at], preferred_element_type=F32)

    for p in range(PARTS):
        for j in far_first(nz)[::-1]:
            pz, device = row_peer(j)
            arrived(rows.at[p, pz], ra.at[p, pz], sa.at[p, j], device)
        run = jnp.zeros((sl, lw), F32)
        for i in range(nz):
            before[p, i] = run
            run = run + rows[p, i].astype(F32)
        total[p] = run.astype(BF16)
        for j in far_first(ny):
            @pl.when(y + j < ny)
            def _():
                send(total.at[p], cols.at[p, y], sb.at[p, j], rb.at[p, y], ((y + j) * nz + z, ten))

    for p in range(PARTS):
        for j in range(1, ny):
            @pl.when(y - j >= 0)
            def _():
                arrived(cols.at[p, y - j], rb.at[p, y - j], sb.at[p, j], ((y - j) * nz + z, ten))
        base = jnp.zeros((sl, lw), F32)
        for i in range(ny):
            base = base + cols[p, i].astype(F32)
        for i in range(nz):
            ready[p, i] = (base + before[p, i]).astype(BF16)
        for j in far_first(nz):
            pz, device = row_peer(j)
            sends.append(send(ready.at[p, pz], prefix.at[p, z], sc.at[p, j], rc.at[p, z], device))
        prefix[p, z] = ready[p, z]

    for p in range(PARTS):
        for j in far_first(nz)[::-1]:
            pz, device = row_peer(j)
            arrived(prefix.at[p, pz], rc.at[p, pz], sc.at[p, j], device)
        for h in range(heads // PARTS):
            at = slice(p * lw + h * DH, p * lw + (h + 1) * DH)
            one = prefix[p, :, :, h * DH:(h + 1) * DH].reshape(DH, DH)
            attn = intra[:, at] + jnp.dot(q[:, at], one, preferred_element_type=F32)
            meansq = jnp.mean(attn * attn, axis=-1, keepdims=True)
            gated[:, at] = (attn * lax.rsqrt(meansq + 1e-05) * g[:, at]).astype(BF16)
        at = pl.ds(p * lw, lw)
        sends.append(send(gated.at[:, at], gated_in.at[:, at], sg.at[p], rg.at[p], partner))

    def product(features, weights, i, part):
        return jnp.dot(features[...], weights[i, :, part * half:(part + 1) * half], preferred_element_type=F32)

    def partial(i, part):
        return product(gated, w, i, part) + product(gated_in, w_in, i, part)

    def there(i):
        wloads[i].wait()
        arrived(w_in.at[i], rw.at[i], sw.at[i], partner)

    there(0)
    own = [product(gated, w, 0, d) for d in range(2)]
    for p in range(PARTS):
        at = pl.ds(p * lw, lw)
        arrived(gated_in.at[:, at], rg.at[p], sg.at[p], partner)
    both = (ahead, behind)
    chunk = tok // CHUNKS
    for d in range(2):
        relay_out[d] = (own[d] + product(gated_in, w_in, 0, d)).astype(BF16)
        for r in range(CHUNKS):
            at = pl.ds(r * chunk, chunk)
            sends.append(send(relay_out.at[d, at], relay_in.at[d, at], sr.at[d, r], rr.at[d, r], both[d]))
    for d in range(2):
        there(1 + d)
        direct_out[d] = partial(1 + d, 1 - d).astype(BF16)
        sends.append(send(direct_out.at[d], direct_in.at[d], sd.at[d], rd.at[d], both[d]))
    terms = [partial(1 + d, d) for d in range(2)]
    for r in range(CHUNKS):
        at = pl.ds(r * chunk, chunk)
        for d in range(2):
            arrived(relay_in.at[d, at], rr.at[d, r], sr.at[d, r], both[1 - d])
            rows_of = slice(r * chunk, (r + 1) * chunk)
            chip_out[d, rows_of] = (terms[d][rows_of] + relay_in[d, rows_of].astype(F32)).astype(BF16)
            sends.append(send(chip_out.at[d, at], chip_in.at[d, at], sx.at[d, r], rx.at[d, r], both[d]))
    there(3)
    own = [partial(3, part) for part in range(2)]
    for d in range(2):
        arrived(direct_in.at[d], rd.at[d], sd.at[d], both[1 - d])
        own[1 - d] = own[1 - d] + direct_in[d].astype(F32)
    for r in range(CHUNKS):
        at = pl.ds(r * chunk, chunk)
        rows_of = slice(r * chunk, (r + 1) * chunk)
        for d in range(2):
            arrived(chip_in.at[d, at], rx.at[d, r], sx.at[d, r], both[1 - d])
            out_ref[rows_of, d * half:(d + 1) * half] = (own[d][rows_of] + chip_in[d, rows_of].astype(F32)).astype(BF16)

    for copy in sends:
        copy.wait_send()
    for p in range(PARTS):
        for j in range(1, ny):
            @pl.when(y + j < ny)
            def _():
                pltpu.make_async_remote_copy(src_ref=total.at[p], dst_ref=cols.at[p, y], send_sem=sb.at[p, j],
                                             recv_sem=rb.at[p, y], device_id=((y + j) * nz + z, ten),
                                             device_id_type=MESH).wait_send()


def solution(mesh):
    n_seq, n_ten = mesh.shape["seq"], mesh.shape["tensor"]
    nz = math.isqrt(n_seq)
    ny, nx = n_seq // nz, n_ten // 2

    def local(query_rows, key_rows, value_rows, block_mask, norm_gain, out_weight):
        tok, feat = query_rows.shape
        width = out_weight.shape[1] // n_ten
        sl, lw = DH // nz, feat // PARTS
        dma = pltpu.SemaphoreType.DMA
        slices = pltpu.VMEM((PARTS, nz, sl, lw), BF16)
        halves = pltpu.VMEM((2, tok, width // 2), BF16)
        return pl.pallas_call(
            functools.partial(kernel, ny, nz, nx),
            out_shape=jax.ShapeDtypeStruct((tok, width), BF16),
            in_specs=[pl.BlockSpec(memory_space=pl.ANY)] * 6,
            out_specs=pl.BlockSpec(memory_space=pltpu.VMEM),
            scratch_shapes=[
                pltpu.VMEM((tok, feat), BF16), pltpu.VMEM((tok, feat), BF16), pltpu.VMEM((tok, feat), BF16),
                pltpu.SMEM((1, 1), jnp.int32), pltpu.VMEM((1, feat), F32),
                pltpu.VMEM((nx, feat, width), BF16), pltpu.VMEM((nx, feat, width), BF16),
                slices, slices, pltpu.VMEM((PARTS, nz, sl, lw), F32), pltpu.VMEM((PARTS, sl, lw), BF16),
                pltpu.VMEM((PARTS, ny, sl, lw), BF16), slices, slices,
                pltpu.VMEM((tok, feat), F32), pltpu.VMEM((tok, feat), BF16), pltpu.VMEM((tok, feat), BF16),
                halves, halves, halves, halves, halves, halves,
                dma((5,)), dma((nx,)), dma((PARTS, nz)), dma((PARTS, nz)), dma((PARTS, ny)), dma((PARTS, ny)),
                dma((PARTS, nz)), dma((PARTS, nz)), dma((nx,)), dma((nx,)), dma((PARTS,)), dma((PARTS,)),
                dma((2, CHUNKS)), dma((2, CHUNKS)), dma((2,)), dma((2,)), dma((2, CHUNKS)), dma((2, CHUNKS)),
            ],
            compiler_params=pltpu.CompilerParams(collective_id=0, has_side_effects=True),
        )(query_rows, key_rows, value_rows, block_mask, norm_gain.reshape(1, feat), out_weight)

    placed = (P("seq", "tensor"), P("seq", "tensor"), P("seq", "tensor"), P("seq", None), P("tensor"), P("tensor", None))
    return jax.shard_map(local, mesh=mesh, in_specs=placed, out_specs=P("seq", "tensor"), check_vma=False)
```

```python
import functools
import math

import jax
import jax.numpy as jnp
from jax import lax
from jax.experimental import pallas as pl
from jax.experimental.pallas import tpu as pltpu
from jax.sharding import PartitionSpec as P

DH = 128
F32, BF16 = jnp.float32, jnp.bfloat16
MESH = pl.DeviceIdType.MESH
PARTS = 2
CHUNKS = 2


def far_first(n):
    return sorted(range(1, n), key=lambda k: -min(k, n - k))


def kernel(ny, nz, nx, q_hbm, k_hbm, v_hbm, m_hbm, g_hbm, w_hbm, out_ref, q, k, v, m, g, w, w_in, state, rows, before, total,
           cols, ready, prefix, intra, gated, gated_in, relay_out, relay_in, direct_out, direct_in, chip_out, chip_in,
           load_sem, wload_sem, sa, ra, sb, rb, sc, rc, sw, rw, sg, rg, sr, rr, sd, rd, sx, rx):
    tok, feat = q.shape
    heads = feat // DH
    sl = DH // nz
    lw = feat // PARTS
    width = w.shape[2]
    half = width // 2
    seq, ten = lax.axis_index("seq"), lax.axis_index("tensor")
    y, z = seq // nz, lax.rem(seq, nz)
    x, c = ten // 2, lax.rem(ten, 2)

    def row_peer(j):
        pz = lax.rem(z + j, nz)
        return pz, (y * nz + pz, ten)

    def col_peer(j):
        py = lax.rem(y + j, ny)
        return py, (py * nz + z, ten)

    def chip_peer(j):
        px = lax.rem(x + j, nx)
        return px, (seq, px * 2 + c)

    partner = (seq, x * 2 + (1 - c))

    cols[...] = jnp.zeros_like(cols)
    barrier = pltpu.get_barrier_semaphore()
    peers = [row_peer(j)[1] for j in far_first(nz)] + [col_peer(j)[1] for j in far_first(ny)]
    ahead, behind = chip_peer(1)[1], chip_peer(nx - 1)[1]
    peers += [ahead, behind, partner]
    for peer in peers:
        pl.semaphore_signal(barrier, inc=1, device_id=peer, device_id_type=MESH)

    loads = [pltpu.make_async_copy(a, b, load_sem.at[i]) for i, (a, b) in enumerate(
        ((k_hbm, k), (v_hbm, v), (q_hbm, q), (m_hbm, m), (g_hbm, g)))]
    for copy in loads:
        copy.start()
    hops = (2, 1, nx - 1, 0)

    def block(i, core):
        px, _ = chip_peer(hops[i])
        return w_hbm.at[:, pl.ds(pl.multiple_of((px * 2 + core) * width, width), width)]

    wloads = [pltpu.make_async_copy(block(i, c), w.at[i], wload_sem.at[i]) for i in range(nx)]
    for copy in wloads:
        copy.start()

    loads[0].wait()
    loads[1].wait()
    for h in range(heads):
        one = lax.dot_general(k[:, h * DH:(h + 1) * DH], v[:, h * DH:(h + 1) * DH], (((0,), (0,)), ((), ())),
                              preferred_element_type=F32)
        part, at = divmod(h * DH, lw)
        state[part, :, :, at:at + DH] = one.astype(BF16).reshape(nz, sl, DH)
    pl.semaphore_wait(barrier, len(peers))

    sends = []

    def send(src, dst, send_sem, recv_sem, device):
        copy = pltpu.make_async_remote_copy(src_ref=src, dst_ref=dst, send_sem=send_sem, recv_sem=recv_sem, device_id=device,
                                            device_id_type=MESH)
        copy.start()
        return copy

    def arrived(dst, recv_sem, send_sem, device):
        pltpu.make_async_remote_copy(src_ref=dst, dst_ref=dst, send_sem=send_sem, recv_sem=recv_sem, device_id=device,
                                     device_id_type=MESH).wait_recv()

    for p in range(PARTS):
        for j in far_first(nz):
            pz, device = row_peer(j)
            sends.append(send(state.at[p, pz], rows.at[p, z], sa.at[p, j], ra.at[p, z], device))
    for p in range(PARTS):
        rows[p, z] = state[p, z]

    for copy in loads[2:]:
        copy.wait()
    row_pos = lax.broadcasted_iota(jnp.int32, (tok, tok), 0)
    col_pos = lax.broadcasted_iota(jnp.int32, (tok, tok), 1)
    allowed = (jnp.full((tok, tok), m[0, 0], jnp.int32) > 0) & (col_pos <= row_pos)
    for h in range(heads):
        at = slice(h * DH, (h + 1) * DH)
        scores = lax.dot_general(q[:, at], k[:, at], (((1,), (1,)), ((), ())), preferred_element_type=F32)
        weights = jnp.where(allowed, scores, 0.0).astype(BF16)
        intra[:, at] = jnp.dot(weights, v[:, at], preferred_element_type=F32)

    for p in range(PARTS):
        for j in far_first(nz)[::-1]:
            pz, device = row_peer(j)
            arrived(rows.at[p, pz], ra.at[p, pz], sa.at[p, j], device)
        run = jnp.zeros((sl, lw), F32)
        for i in range(nz):
            before[p, i] = run
            run = run + rows[p, i].astype(F32)
        total[p] = run.astype(BF16)
        for j in far_first(ny):
            @pl.when(y + j < ny)
            def _():
                send(total.at[p], cols.at[p, y], sb.at[p, j], rb.at[p, y], ((y + j) * nz + z, ten))

    for i in range(nx):
        sends.append(send(block(i, 1 - c), w_in.at[i], sw.at[i], rw.at[i], partner))
    for p in range(PARTS):
        for j in range(1, ny):
            @pl.when(y - j >= 0)
            def _():
                arrived(cols.at[p, y - j], rb.at[p, y - j], sb.at[p, j], ((y - j) * nz + z, ten))
        base = jnp.zeros((sl, lw), F32)
        for i in range(ny):
            base = base + cols[p, i].astype(F32)
        for i in range(nz):
            ready[p, i] = (base + before[p, i]).astype(BF16)
        for j in far_first(nz):
            pz, device = row_peer(j)
            sends.append(send(ready.at[p, pz], prefix.at[p, z], sc.at[p, j], rc.at[p, z], device))
        prefix[p, z] = ready[p, z]

    for p in range(PARTS):
        for j in far_first(nz)[::-1]:
            pz, device = row_peer(j)
            arrived(prefix.at[p, pz], rc.at[p, pz], sc.at[p, j], device)
        for h in range(heads // PARTS):
            at = slice(p * lw + h * DH, p * lw + (h + 1) * DH)
            one = prefix[p, :, :, h * DH:(h + 1) * DH].reshape(DH, DH)
            attn = intra[:, at] + jnp.dot(q[:, at], one, preferred_element_type=F32)
            meansq = jnp.mean(attn * attn, axis=-1, keepdims=True)
            gated[:, at] = (attn * lax.rsqrt(meansq + 1e-05) * g[:, at]).astype(BF16)
        at = pl.ds(p * lw, lw)
        sends.append(send(gated.at[:, at], gated_in.at[:, at], sg.at[p], rg.at[p], partner))

    def product(features, weights, i, part):
        return jnp.dot(features[...], weights[i, :, part * half:(part + 1) * half], preferred_element_type=F32)

    def partial(i, part):
        return product(gated, w, i, part) + product(gated_in, w_in, i, part)

    def there(i):
        wloads[i].wait()
        arrived(w_in.at[i], rw.at[i], sw.at[i], partner)

    there(0)
    own = [product(gated, w, 0, d) for d in range(2)]
    for p in range(PARTS):
        at = pl.ds(p * lw, lw)
        arrived(gated_in.at[:, at], rg.at[p], sg.at[p], partner)
    both = (ahead, behind)
    chunk = tok // CHUNKS
    for d in range(2):
        relay_out[d] = (own[d] + product(gated_in, w_in, 0, d)).astype(BF16)
        for r in range(CHUNKS):
            at = pl.ds(r * chunk, chunk)
            sends.append(send(relay_out.at[d, at], relay_in.at[d, at], sr.at[d, r], rr.at[d, r], both[d]))
    for d in range(2):
        there(1 + d)
        direct_out[d] = partial(1 + d, 1 - d).astype(BF16)
        sends.append(send(direct_out.at[d], direct_in.at[d], sd.at[d], rd.at[d], both[d]))
    terms = [partial(1 + d, d) for d in range(2)]
    for r in range(CHUNKS):
        at = pl.ds(r * chunk, chunk)
        for d in range(2):
            arrived(relay_in.at[d, at], rr.at[d, r], sr.at[d, r], both[1 - d])
            rows_of = slice(r * chunk, (r + 1) * chunk)
            chip_out[d, rows_of] = (terms[d][rows_of] + relay_in[d, rows_of].astype(F32)).astype(BF16)
            sends.append(send(chip_out.at[d, at], chip_in.at[d, at], sx.at[d, r], rx.at[d, r], both[d]))
    there(3)
    own = [partial(3, part) for part in range(2)]
    for d in range(2):
        arrived(direct_in.at[d], rd.at[d], sd.at[d], both[1 - d])
        own[1 - d] = own[1 - d] + direct_in[d].astype(F32)
    for r in range(CHUNKS):
        at = pl.ds(r * chunk, chunk)
        rows_of = slice(r * chunk, (r + 1) * chunk)
        for d in range(2):
            arrived(chip_in.at[d, at], rx.at[d, r], sx.at[d, r], both[1 - d])
            out_ref[rows_of, d * half:(d + 1) * half] = (own[d][rows_of] + chip_in[d, rows_of].astype(F32)).astype(BF16)

    for copy in sends:
        copy.wait_send()
    for p in range(PARTS):
        for j in range(1, ny):
            @pl.when(y + j < ny)
            def _():
                pltpu.make_async_remote_copy(src_ref=total.at[p], dst_ref=cols.at[p, y], send_sem=sb.at[p, j],
                                             recv_sem=rb.at[p, y], device_id=((y + j) * nz + z, ten),
                                             device_id_type=MESH).wait_send()


def solution(mesh):
    n_seq, n_ten = mesh.shape["seq"], mesh.shape["tensor"]
    nz = math.isqrt(n_seq)
    ny, nx = n_seq // nz, n_ten // 2

    def local(query_rows, key_rows, value_rows, block_mask, norm_gain, out_weight):
        tok, feat = query_rows.shape
        width = out_weight.shape[1] // n_ten
        sl, lw = DH // nz, feat // PARTS
        dma = pltpu.SemaphoreType.DMA
        slices = pltpu.VMEM((PARTS, nz, sl, lw), BF16)
        halves = pltpu.VMEM((2, tok, width // 2), BF16)
        return pl.pallas_call(
            functools.partial(kernel, ny, nz, nx),
            out_shape=jax.ShapeDtypeStruct((tok, width), BF16),
            in_specs=[pl.BlockSpec(memory_space=pl.ANY)] * 6,
            out_specs=pl.BlockSpec(memory_space=pltpu.VMEM),
            scratch_shapes=[
                pltpu.VMEM((tok, feat), BF16), pltpu.VMEM((tok, feat), BF16), pltpu.VMEM((tok, feat), BF16),
                pltpu.SMEM((1, 1), jnp.int32), pltpu.VMEM((1, feat), F32),
                pltpu.VMEM((nx, feat, width), BF16), pltpu.VMEM((nx, feat, width), BF16),
                slices, slices, pltpu.VMEM((PARTS, nz, sl, lw), F32), pltpu.VMEM((PARTS, sl, lw), BF16),
                pltpu.VMEM((PARTS, ny, sl, lw), BF16), slices, slices,
                pltpu.VMEM((tok, feat), F32), pltpu.VMEM((tok, feat), BF16), pltpu.VMEM((tok, feat), BF16),
                halves, halves, halves, halves, halves, halves,
                dma((5,)), dma((nx,)), dma((PARTS, nz)), dma((PARTS, nz)), dma((PARTS, ny)), dma((PARTS, ny)),
                dma((PARTS, nz)), dma((PARTS, nz)), dma((nx,)), dma((nx,)), dma((PARTS,)), dma((PARTS,)),
                dma((2, CHUNKS)), dma((2, CHUNKS)), dma((2,)), dma((2,)), dma((2, CHUNKS)), dma((2, CHUNKS)),
            ],
            compiler_params=pltpu.CompilerParams(collective_id=0, has_side_effects=True),
        )(query_rows, key_rows, value_rows, block_mask, norm_gain.reshape(1, feat), out_weight)

    placed = (P("seq", "tensor"), P("seq", "tensor"), P("seq", "tensor"), P("seq", None), P("tensor"), P("tensor", None))
    return jax.shard_map(local, mesh=mesh, in_specs=placed, out_specs=P("seq", "tensor"), check_vma=False)
```
